32 devices in a mesh: dp: 4 (over y, x), fsdp: 8 (over z, core).
Axes of the slice: x: 2, y: 2, z: 4, core: 2. Of those that a mesh axis runs over, the one named last changes fastest.
Arguments:
- hidden: bfloat16 [16384, 1536], P(('dp', 'fsdp')), may hold values from -6 to 6
- lengths: int32 [512], P(('dp', 'fsdp')), may hold values from 1 to 32
- norm_gain: float32 [1536], replicated, may hold values from 0.1 to 1.9
- up_weight: bfloat16 [1536, 3072], P('fsdp'), may hold values from -0.15625 to 0.15625
- down_weight: bfloat16 [3072, 1536], P('fsdp'), may hold values from -0.109375 to 0.109375
- pool_gain: float32 [1536], replicated, may hold values from 0.1 to 1.9
- proj_weight: bfloat16 [1536, 768], P('fsdp'), may hold values from -1 to 1
- owners: int32 [512, 1], P(('dp', 'fsdp')), may hold values from 0 to 3; in each aligned block of 16 rows (0 to 15, 16 to 31, ...) at most 8 rows name the same one
Outputs:
- owned: bfloat16 [1024, 768], P(('dp', 'fsdp'))
The draws below stay inside these ranges and needn't reach their ends.
Inputs may be any that keep to these rules, and one draw needn't show every extreme that they name: `owners`: in each aligned block of 16 passages no owner is named by more than 8 passages, a bound that some block reaches.
All inputs are finite; a program needn't handle non-finite values.
Results may differ from the reference program's by a relative error of at most 0.014.
Values may be sent and summed in bfloat16 or wider, within the bound.
A program may use at most 128 MiB of HBM per device.

```python
import math
import jax
import jax.numpy as jnp
import numpy as np
from jax import lax

D = 1536
FF = 3072
E = 768
LEN = 32
PASS_DEV = 16
ITERS = 4
PASSAGES = 512
CAP = 8
N_DP = 4
N_FSDP = 8


def draw_proj_weight(key, part):
    entry_key, scale_key = jax.random.split(jax.random.fold_in(key, 7))
    entries = jax.random.truncated_normal(entry_key, -3.0, 3.0, (D, E), jnp.float32)
    column_scale = jnp.exp(jax.random.uniform(scale_key, (E,), jnp.float32, math.log(0.3), math.log(3.0)))
    scaled = entries * column_scale[None, :] * (1.0 / math.sqrt(D))
    return jnp.clip(scaled, -1.0, 1.0).astype(jnp.bfloat16)


def place_ends(values, key, least, top_value):
    extent = values.shape
    index_at = [jax.random.randint(jax.random.fold_in(key, axis), (), 0, extent[axis]) for axis in range(len(extent))]
    values = values.at[tuple(index_at)].set(least)
    longest = extent.index(max(extent))
    index_at[longest] = (index_at[longest] + 1) % extent[longest]
    return values.at[tuple(index_at)].set(top_value)


def level_of(rng, shape, cuts, least, top_value):
    factor_of = 1.0
    for dim, parts in cuts:
        heights = jax.random.uniform(jax.random.fold_in(jax.random.fold_in(rng, 6), dim), (parts,), jnp.float32, least / len(cuts), top_value / len(cuts))
        factor_of = factor_of * jnp.repeat(jnp.exp(heights), shape[dim] // parts).reshape((-1,) + (1,) * (len(shape) - 1 - dim))
    return factor_of


def assign_block(own_key, own, number, rows, count, top, limit, slope):
    ranking = jax.random.permutation(own_key, count)
    crowded, usual = portions_of(count, rows * top, limit, slope, True), portions_of(count, rows * top, limit, slope, False)
    places = jnp.arange(count)

    def named(sizes, rotation):
        used = int((sizes > 0).sum())
        fixed = max(1, used // 4)
        shifted = fixed + (places - fixed + rotation * (used - fixed)) % max(1, count - fixed)
        return jnp.zeros((count,), jnp.int32).at[ranking[jnp.where(places < fixed, places, shifted)]].set(jnp.asarray(sizes, jnp.int32))

    sizes = jnp.where(number % 4 == 0, named(crowded, number // 4), named(usual, number - number // 4 - 1))
    mixed = jax.random.permutation(jax.random.fold_in(own, 3), count)
    giver, receiver = mixed[0:count // 2 * 2:2], mixed[1:count // 2 * 2:2]
    slack = jnp.minimum(sizes[giver] - 1, limit - sizes[receiver]) // 2
    slack = jnp.where((giver == ranking[0]) | (receiver == ranking[0]) | (sizes[receiver] == 0), 0, jnp.maximum(slack, 0))
    shifted = jax.random.randint(jax.random.fold_in(own, 4), (count // 2,), 0, 1 << 20) % (slack + 1)
    sizes = sizes.at[giver].add(-shifted).at[receiver].add(shifted)
    labels = jnp.searchsorted(jnp.cumsum(sizes), jnp.arange(rows * top), side="right").astype(jnp.int32)
    grid = labels.reshape(top, rows).T
    grid = grid[jax.random.permutation(jax.random.fold_in(own, 1), rows)]
    rotation = jax.random.randint(jax.random.fold_in(own, 2), (rows, 1), 0, top)
    return jnp.take_along_axis(grid, (jnp.arange(top)[None, :] + rotation) % top, axis=1)


def portions_of(count, total, reach, lean, full):
    loads = [(1 << 20) // math.isqrt(grade ** lean) + 1 for grade in range(1, count + 1)]
    largest = reach if full else min(reach, max(-(-total // count), total * loads[0] // sum(loads)))
    least = 1 if total - largest >= count - 1 else 0
    counts, spare = [largest] + [least] * (count - 1), total - largest - least * (count - 1)
    while spare > 0:
        candidates = [i for i in range(1, count) if counts[i] < largest] or [i for i in range(1, count) if counts[i] < reach]
        mass, left = sum([loads[i] for i in candidates]), spare
        for i in candidates:
            addition = min(reach - counts[i], max(1, left * loads[i] // mass), spare)
            counts[i] = counts[i] + addition
            spare = spare - addition
    return np.array(counts)


def gaussian(own_key, dims, scale, reach, shards=(), kind=jnp.bfloat16):
    values = jax.random.normal(own_key, dims, jnp.float32) * scale
    if len(shards) > 0:
        values = level_of(own_key, dims, shards, -0.22, 0.18) * values
    return jnp.clip(values, min=-reach, max=reach).astype(kind)


def setup_inputs(seed: int = 0) -> dict:
    splits = jax.random.split(jax.random.key(seed), 9)
    hidden = gaussian(splits[0], (PASSAGES * LEN, D), 1.0, 6.0, ((0, 32),))
    lengths = place_ends(jax.random.randint(splits[1], (PASSAGES,), 1, LEN + 1), jax.random.fold_in(splits[1], 1), 1, LEN).astype(jnp.int32)
    norm_gain = jnp.clip(1.0 + 0.18 * jax.random.normal(splits[2], (D,), jnp.float32), 0.1, 1.9)
    up_weight = gaussian(splits[3], (D, FF), D ** -0.5, 0.15625, ((0, 8),))
    down_weight = gaussian(splits[4], (FF, D), FF ** -0.5, 0.109375, ((0, 8),))
    pool_gain = jnp.clip(1.0 + 0.18 * jax.random.normal(splits[5], (D,), jnp.float32), 0.1, 1.9)
    proj_weight = draw_proj_weight(jax.random.fold_in(splits[8], 71), 0)
    owners_keys = jax.random.split(jax.random.fold_in(splits[7], 1), PASSAGES // PASS_DEV)
    owners_turns = jax.random.permutation(jax.random.fold_in(splits[7], 3), PASSAGES // PASS_DEV)
    owners = jax.vmap(lambda own, number: assign_block(jax.random.fold_in(splits[7], 2), own, number, PASS_DEV, N_DP, 1, CAP, 1))(owners_keys, owners_turns).reshape((PASSAGES, 1))
    return dict(hidden=hidden, lengths=lengths, norm_gain=norm_gain, up_weight=up_weight, down_weight=down_weight, pool_gain=pool_gain, proj_weight=proj_weight, owners=owners)


RIDGE_TERM = 1.0
EPSILON = 1e-06
PRECISE = lax.Precision.HIGHEST

def rms_scale(values, gain_vector):
    return values * lax.rsqrt(lax.optimization_barrier(jnp.mean(values * values, axis=-1, keepdims=True)) + EPSILON) * gain_vector

def build_covariance(full_sums, average_sum, row_count):
    average = average_sum / row_count
    eye_matrix = jnp.eye(full_sums.shape[0], dtype=full_sums.dtype)
    covariance = full_sums / row_count - average[:, None] * average[None, :] + RIDGE_TERM * eye_matrix
    magnitude = jnp.sqrt(jnp.sum(covariance * covariance))
    initial = 4.0 / magnitude * eye_matrix - 4.0 * covariance / (magnitude * magnitude)
    return (covariance, average, initial)

def newton_update(iterate_rows, covariance, iterate_full):
    mixed = jnp.dot(jnp.dot(iterate_rows, covariance, precision=PRECISE, preferred_element_type=jnp.float32), iterate_full, precision=PRECISE, preferred_element_type=jnp.float32)
    return 2.0 * iterate_rows - mixed

def reference(hidden, lengths, norm_gain, up_weight, down_weight, pool_gain, proj_weight, owners):
    group_pass = PASS_DEV * N_FSDP

    def pool_block(inputs):
        row_block, block_lengths = inputs
        normed = rms_scale(row_block.astype(jnp.float32), norm_gain).astype(jnp.bfloat16)
        hidden_pre = jnp.dot(normed, up_weight, preferred_element_type=jnp.float32)
        activated = jax.nn.gelu(hidden_pre, approximate=True).astype(jnp.bfloat16)
        layer_out = (row_block.astype(jnp.float32) + jnp.dot(activated, down_weight, preferred_element_type=jnp.float32)).astype(jnp.bfloat16)
        grouped = layer_out.astype(jnp.float32).reshape(group_pass, LEN, D)
        keep_mask = (jnp.arange(LEN)[None, :] < block_lengths[:, None]).astype(jnp.float32)
        summed = lax.optimization_barrier(jnp.sum(grouped * keep_mask[:, :, None], axis=1))
        return summed / block_lengths.astype(jnp.float32)[:, None]
    pooled = lax.map(pool_block, (hidden.reshape(N_DP, group_pass * LEN, D), lengths.reshape(N_DP, group_pass)))
    pooled = pooled.reshape(PASSAGES, D)
    pool_normed = rms_scale(pooled, pool_gain).astype(jnp.bfloat16)
    embedded = jnp.dot(pool_normed, proj_weight, preferred_element_type=jnp.float32)
    products = jnp.dot(embedded.T, embedded, precision=PRECISE, preferred_element_type=jnp.float32)
    column_sum = lax.optimization_barrier(jnp.sum(embedded, axis=0))
    covariance, average, iterate_full = build_covariance(products, column_sum, float(PASSAGES))
    for iteration in range(ITERS - 1):
        iterate_full = newton_update(iterate_full, covariance, iterate_full)
    whitened = jnp.dot(embedded - average, iterate_full, precision=PRECISE, preferred_element_type=jnp.float32).astype(jnp.bfloat16)

    def route_block(row_values, target_owner):
        position = jnp.arange(PASS_DEV)
        earlier = (target_owner[:, None] == target_owner[None, :]) & (position[None, :] < position[:, None])
        target = target_owner * CAP + lax.optimization_barrier(jnp.sum(earlier.astype(jnp.int32), axis=1))
        selector = (jnp.arange(N_DP * CAP)[:, None] == target[None, :]).astype(jnp.bfloat16)
        return jnp.dot(selector, row_values, preferred_element_type=jnp.float32).astype(jnp.bfloat16)
    row_groups = whitened.reshape(N_DP * N_FSDP, PASS_DEV, E)
    owner_groups = owners.reshape(N_DP * N_FSDP, PASS_DEV)
    buffers = jax.vmap(route_block)(row_groups, owner_groups)
    buffers = buffers.reshape(N_DP, N_FSDP, N_DP, CAP, E).transpose(2, 1, 0, 3, 4)
    return buffers.reshape(N_DP * N_FSDP * N_DP * CAP, E)
```

```python
import jax
import jax.numpy as jnp
from jax import lax
from jax.sharding import PartitionSpec as P

RIDGE_TERM = 1.0
EPSILON = 1e-06
HIGH = lax.Precision.HIGH


def fdot(a, b):
    return jnp.dot(a, b, precision=HIGH, preferred_element_type=jnp.float32)


def exchange(blocks):
    return lax.all_to_all(blocks, "fsdp", split_axis=0, concat_axis=0, tiled=True)


def on_device(hidden, lengths, norm_gain, up_weight, down_weight, pool_gain, proj_weight, owners):
    tok_rows, width = hidden.shape
    pass_rows = lengths.shape[0]
    seq_len = tok_rows // pass_rows
    n_fsdp = lax.axis_size("fsdp")
    n_dp = lax.axis_size("dp")
    me = lax.axis_index("fsdp")
    ff_rows = down_weight.shape[0]
    d_rows, emb = proj_weight.shape
    group = n_fsdp * pass_rows
    hidden32 = hidden.astype(jnp.float32)
    normed = (
        hidden32
        * lax.rsqrt(jnp.mean(hidden32 * hidden32, axis=-1, keepdims=True) + EPSILON)
        * norm_gain
    ).astype(jnp.bfloat16)
    hidden_pre = jnp.dot(
        normed,
        lax.all_gather(up_weight, "fsdp", axis=0, tiled=True),
        preferred_element_type=jnp.float32,
    )
    activated = jax.nn.gelu(hidden_pre, approximate=True).astype(jnp.bfloat16)
    token_index = lax.broadcasted_iota(jnp.int32, (pass_rows, tok_rows), 1)
    passage_index = lax.broadcasted_iota(jnp.int32, (pass_rows, tok_rows), 0)
    inside = (
        (token_index // seq_len == passage_index) & (token_index % seq_len < lengths[:, None])
    ).astype(jnp.bfloat16)
    inverse = 1.0 / lengths.astype(jnp.float32)[:, None]
    act_mean = jnp.dot(inside, activated, preferred_element_type=jnp.float32) * inverse
    hid_mean = jnp.dot(inside, hidden, preferred_element_type=jnp.float32) * inverse
    packed = jnp.concatenate(
        [
            act_mean.reshape(pass_rows, n_fsdp, ff_rows),
            hid_mean.reshape(pass_rows, n_fsdp, d_rows),
        ],
        axis=2,
    ).transpose(1, 0, 2)
    pooled_in = exchange(packed).reshape(group, ff_rows + d_rows)
    partial = fdot(pooled_in[:, :ff_rows], down_weight.astype(jnp.float32))
    partial = partial.reshape(group, n_fsdp, d_rows).transpose(1, 0, 2)
    pooled = jnp.sum(exchange(partial), axis=0) + pooled_in[:, ff_rows:]
    squares = jnp.sum(pooled * pooled, axis=1, keepdims=True)
    gain = lax.dynamic_slice(pool_gain, (me * d_rows,), (d_rows,))
    emb_part = fdot(pooled * gain, proj_weight.astype(jnp.float32))
    emb_part = jnp.concatenate([emb_part, jnp.broadcast_to(squares, (group, 128))], axis=1)
    summed = jnp.sum(exchange(emb_part.reshape(n_fsdp, pass_rows, emb + 128)), axis=0)
    embedded = summed[:, :emb] * lax.rsqrt(summed[:, emb : emb + 1] / width + EPSILON)
    everyone = lax.all_gather(embedded, ("dp", "fsdp"), axis=0, tiled=True)
    total_rows = float(everyone.shape[0])
    average = jnp.sum(everyone, axis=0) / total_rows
    eye = jnp.eye(emb, dtype=jnp.float32)
    covariance = (
        fdot(everyone.T, everyone) / total_rows
        - average[:, None] * average[None, :]
        + RIDGE_TERM * eye
    )
    magnitude = jnp.sqrt(jnp.sum(covariance * covariance))
    s1 = eye - (2.0 / magnitude) * covariance
    s2 = fdot(s1, s1)
    s4 = fdot(s2, s2)
    rows = (embedded - average) * (2.0 / magnitude)
    rows = rows + fdot(rows, s1)
    rows = rows + fdot(rows, s2)
    rows = rows + fdot(rows, s4)
    rows = rows + fdot(fdot(rows, s4), s4)
    whitened = rows.astype(jnp.bfloat16)
    capacity = 2 * pass_rows // n_dp
    target_owner = owners[:, 0]
    position = lax.broadcasted_iota(jnp.int32, (pass_rows, pass_rows), 0)
    previous = lax.broadcasted_iota(jnp.int32, (pass_rows, pass_rows), 1)
    earlier = (target_owner[:, None] == target_owner[None, :]) & (previous < position)
    target = target_owner * capacity + jnp.sum(earlier.astype(jnp.int32), axis=1)
    slot_index = lax.broadcasted_iota(jnp.int32, (n_dp * capacity, pass_rows), 0)
    selector = (slot_index == target[None, :]).astype(jnp.bfloat16)
    outgoing = jnp.dot(selector, whitened, preferred_element_type=jnp.float32).astype(jnp.bfloat16)
    return lax.all_to_all(outgoing, "dp", split_axis=0, concat_axis=0, tiled=True)


def solution(mesh):
    placed = (
        P(("dp", "fsdp"), None),
        P(("dp", "fsdp")),
        P(),
        P("fsdp", None),
        P("fsdp", None),
        P(),
        P("fsdp", None),
        P(("dp", "fsdp"), None),
    )
    return jax.shard_map(
        on_device, mesh=mesh, in_specs=placed, out_specs=P(("dp", "fsdp"), None), check_vma=False
    )
```

```python
import functools

import jax
import jax.numpy as jnp
from jax import lax
from jax.experimental import pallas as pl
from jax.experimental.pallas import tpu as pltpu
from jax.sharding import PartitionSpec as P

RIDGE_TERM = 1.0
EPSILON = 1e-06
HIGH = lax.Precision.HIGH


def fdot(a, b):
    return jnp.dot(a, b, precision=HIGH, preferred_element_type=jnp.float32)


MESH = pl.DeviceIdType.MESH
PLANE = 4


def remote(src, dst, send, recv, device):
    return pltpu.make_async_remote_copy(
        src_ref=src, dst_ref=dst, send_sem=send, recv_sem=recv, device_id=device, device_id_type=MESH
    )


def meet(devices):
    barrier = pltpu.get_barrier_semaphore()
    for device in devices:
        pl.semaphore_signal(barrier, inc=1, device_id=device, device_id_type=MESH)
    pl.semaphore_wait(barrier, len(devices))


def mate(q, e):
    if e == 1:
        return q + 1 - 2 * (q % 2)
    if e == 2:
        return q + 2 - 4 * (q // 2)
    return 3 - q


def gather_kernel(
    nz, up_ref, full_ref, own_sem, z_send, z_recv, p_send, p_recv, x_send, x_recv, f_send, f_recv
):
    i = lax.axis_index("dp")
    j = lax.axis_index("fsdp")
    z = j // 2
    c = j % 2
    q = i % PLANE
    base = i - q
    rows = up_ref.shape[0]
    cols = up_ref.shape[1] // PLANE

    def row_at(level):
        return pl.ds(pl.multiple_of((level * 2 + c) * rows, rows), rows)

    def col_at(part):
        return pl.ds(pl.multiple_of(part * cols, cols), cols)

    partner = (i, z * 2 + 1 - c)
    z_peers = [(i, ((z + d) % nz) * 2 + c) for d in range(1, nz)]
    mates = [(base + mate(q, e), j) for e in range(1, PLANE)]
    meet([partner] + z_peers + mates)
    own = pltpu.make_async_copy(up_ref, full_ref.at[row_at(z), :], own_sem)
    pending = []

    def send(src, dst, ssem, rsem, device):
        copy = remote(src, dst, ssem, rsem, device)
        copy.start()
        pending.append(copy)
        return copy

    z_copies = [
        send(
            up_ref.at[:, col_at(q)], full_ref.at[row_at(z), col_at(q)], z_send.at[d], z_recv.at[d], peer
        )
        for d, peer in enumerate(z_peers)
    ]
    own.start()
    p_copies = [send(up_ref, full_ref.at[row_at(z), :], p_send, p_recv, partner)]
    x_copies = []
    for d in range(nz - 1):
        z_copies[d].wait_recv()
        piece = full_ref.at[row_at((z + nz - d - 1) % nz), col_at(q)]
        for e in range(PLANE - 1):
            n = d * (PLANE - 1) + e
            x_copies.append(send(piece, piece, x_send.at[n], x_recv.at[n], mates[e]))
        n = d * PLANE + PLANE - 1
        p_copies.append(send(piece, piece, f_send.at[n], f_recv.at[n], partner))
    for d in range(nz - 1):
        for e in range(PLANE - 1):
            x_copies[d * (PLANE - 1) + e].wait_recv()
            piece = full_ref.at[row_at((z + nz - d - 1) % nz), col_at(mate(q, e + 1))]
            n = d * PLANE + e
            p_copies.append(send(piece, piece, f_send.at[n], f_recv.at[n], partner))
    for copy in p_copies:
        copy.wait_recv()
    for copy in pending:
        copy.wait_send()
    own.wait()


def gather_up(up_weight, n_fsdp):
    rows, cols = up_weight.shape
    nz = n_fsdp // 2
    dma = pltpu.SemaphoreType.DMA
    return pl.pallas_call(
        functools.partial(gather_kernel, nz),
        out_shape=jax.ShapeDtypeStruct((rows * n_fsdp, cols), up_weight.dtype),
        in_specs=[pl.BlockSpec(memory_space=pl.ANY)],
        out_specs=pl.BlockSpec(memory_space=pl.ANY),
        scratch_shapes=[
            dma,
            dma((nz - 1,)),
            dma((nz - 1,)),
            dma,
            dma,
            dma(((nz - 1) * (PLANE - 1),)),
            dma(((nz - 1) * (PLANE - 1),)),
            dma(((nz - 1) * PLANE,)),
            dma(((nz - 1) * PLANE,)),
        ],
        compiler_params=pltpu.CompilerParams(collective_id=0, has_side_effects=True),
        name="gather_up",
    )(up_weight)


def mix_kernel(
    n_dp, n_fsdp, width,
    a_ref, h_ref, down_ref, proj_ref, gain_ref, emb_ref, all_ref,
    ra, rh, s2, r2, s3, r3,
    as_, ar, hs, hr, s2s, r2s, s3s, r3s, es, er, ps, pr,
):
    i = lax.axis_index("dp")
    j = lax.axis_index("fsdp")
    peers = [(j + d) % n_fsdp for d in range(1, n_fsdp)]
    planes = [(i + e) % n_dp for e in range(1, n_dp)]
    pass_rows, ff_rows = a_ref.shape[1:]
    d_rows = h_ref.shape[2]
    emb = proj_ref.shape[1]
    group = n_fsdp * pass_rows
    meet([(i, p) for p in peers] + [(p, j) for p in planes])
    pending = []

    def send(src, dst, ssem, rsem, device):
        copy = remote(src, dst, ssem, rsem, device)
        copy.start()
        pending.append(copy)
        return copy

    first = []
    second = []
    for d, p in enumerate(peers):
        first.append(send(a_ref.at[p], ra.at[j], as_.at[d], ar.at[d], (i, p)))
        second.append(send(h_ref.at[p], rh.at[j], hs.at[d], hr.at[d], (i, p)))
    ra[j] = a_ref[j]
    rh[j] = h_ref[j]
    for copy in first:
        copy.wait_recv()
    acts = ra[...].reshape(group, ff_rows)
    parts = []
    for d, p in enumerate(peers):
        s2[d] = jnp.dot(acts, down_ref[p], preferred_element_type=jnp.float32).astype(s2.dtype)
        parts.append(send(s2.at[d], r2.at[d], s2s.at[d], r2s.at[d], (i, p)))
    pooled = jnp.dot(acts, down_ref[j], preferred_element_type=jnp.float32)
    for copy in second:
        copy.wait_recv()
    pooled = pooled + rh[...].astype(jnp.float32).reshape(group, d_rows)
    for d, copy in enumerate(parts):
        copy.wait_recv()
        pooled = pooled + r2[d].astype(jnp.float32)
    squares = jnp.sum(pooled * pooled, axis=1, keepdims=True)
    scaled = (pooled * gain_ref[...]).astype(proj_ref.dtype)
    part = jnp.dot(scaled, proj_ref[...], preferred_element_type=jnp.float32)
    s3[:, :, :emb] = part.astype(s3.dtype).reshape(n_fsdp, pass_rows, emb)
    wide = jnp.broadcast_to(squares, (group, 128))
    high = wide.astype(s3.dtype)
    low = (wide - high.astype(jnp.float32)).astype(s3.dtype)
    s3[:, :, emb : emb + 128] = high.reshape(n_fsdp, pass_rows, 128)
    s3[:, :, emb + 128 : emb + 256] = low.reshape(n_fsdp, pass_rows, 128)
    third = [
        send(s3.at[p], r3.at[d], s3s.at[d], r3s.at[d], (i, p)) for d, p in enumerate(peers)
    ]
    total = s3[j].astype(jnp.float32)
    for d, copy in enumerate(third):
        copy.wait_recv()
        total = total + r3[d].astype(jnp.float32)
    norm = (total[:, emb : emb + 1] + total[:, emb + 128 : emb + 129]) / width
    embedded = total[:, :emb] * lax.rsqrt(norm + EPSILON)
    emb_ref[...] = embedded
    all_ref[i, j] = embedded.astype(all_ref.dtype)
    mine = all_ref.at[i, j]
    fourth = [send(mine, mine, es.at[d], er.at[d], (i, p)) for d, p in enumerate(peers)]
    for copy in fourth:
        copy.wait_recv()
    block = all_ref.at[i]
    fifth = [send(block, block, ps.at[e], pr.at[e], (p, j)) for e, p in enumerate(planes)]
    for copy in fifth:
        copy.wait_recv()
    for copy in pending:
        copy.wait_send()


def mix(acts, hid, down, proj, gain, n_dp):
    n_fsdp, pass_rows, ff_rows = acts.shape
    d_rows, emb = proj.shape
    group = n_fsdp * pass_rows
    bf = jnp.bfloat16
    dma = pltpu.SemaphoreType.DMA
    vmem = pl.BlockSpec(memory_space=pltpu.VMEM)
    near = [dma((n_fsdp - 1,))] * 2
    return pl.pallas_call(
        functools.partial(mix_kernel, n_dp, n_fsdp, float(n_fsdp * d_rows)),
        out_shape=(
            jax.ShapeDtypeStruct((pass_rows, emb), jnp.float32),
            jax.ShapeDtypeStruct((n_dp, n_fsdp, pass_rows, emb), bf),
        ),
        in_specs=[vmem] * 5,
        out_specs=(vmem, vmem),
        scratch_shapes=[
            pltpu.VMEM((n_fsdp, pass_rows, ff_rows), bf),
            pltpu.VMEM((n_fsdp, pass_rows, d_rows), bf),
            pltpu.VMEM((n_fsdp - 1, group, d_rows), bf),
            pltpu.VMEM((n_fsdp - 1, group, d_rows), bf),
            pltpu.VMEM((n_fsdp, pass_rows, emb + 256), bf),
            pltpu.VMEM((n_fsdp - 1, pass_rows, emb + 256), bf),
        ]
        + near * 5
        + [dma((n_dp - 1,))] * 2,
        compiler_params=pltpu.CompilerParams(
            collective_id=1, has_side_effects=True, vmem_limit_bytes=40 * 1024 * 1024
        ),
        name="mix",
    )(acts, hid, down, proj, gain)


def on_device(hidden, lengths, norm_gain, up_weight, down_weight, pool_gain, proj_weight, owners):
    tok_rows, width = hidden.shape
    pass_rows = lengths.shape[0]
    seq_len = tok_rows // pass_rows
    n_fsdp = lax.axis_size("fsdp")
    n_dp = lax.axis_size("dp")
    me = lax.axis_index("fsdp")
    ff_rows = down_weight.shape[0]
    d_rows, emb = proj_weight.shape
    group = n_fsdp * pass_rows
    hidden32 = hidden.astype(jnp.float32)
    normed = (
        hidden32
        * lax.rsqrt(jnp.mean(hidden32 * hidden32, axis=-1, keepdims=True) + EPSILON)
        * norm_gain
    ).astype(jnp.bfloat16)
    hidden_pre = jnp.dot(
        normed,
        gather_up(up_weight, n_fsdp),
        preferred_element_type=jnp.float32,
    )
    activated = jax.nn.gelu(hidden_pre, approximate=True).astype(jnp.bfloat16)
    token_index = lax.broadcasted_iota(jnp.int32, (pass_rows, tok_rows), 1)
    passage_index = lax.broadcasted_iota(jnp.int32, (pass_rows, tok_rows), 0)
    inside = (
        (token_index // seq_len == passage_index) & (token_index % seq_len < lengths[:, None])
    ).astype(jnp.bfloat16)
    inverse = 1.0 / lengths.astype(jnp.float32)[:, None]
    act_mean = jnp.dot(inside, activated, preferred_element_type=jnp.float32) * inverse
    hid_mean = jnp.dot(inside, hidden, preferred_element_type=jnp.float32) * inverse
    acts = act_mean.astype(jnp.bfloat16).reshape(pass_rows, n_fsdp, ff_rows).transpose(1, 0, 2)
    hid = hid_mean.astype(jnp.bfloat16).reshape(pass_rows, n_fsdp, d_rows).transpose(1, 0, 2)
    down = down_weight.reshape(ff_rows, n_fsdp, d_rows).transpose(1, 0, 2)
    gain = lax.dynamic_slice(pool_gain, (me * d_rows,), (d_rows,))[None, :]
    embedded, everyone = mix(acts, hid, down, proj_weight, gain, n_dp)
    everyone = everyone.reshape(n_dp * group, emb)
    total_rows = float(everyone.shape[0])
    average = jnp.sum(everyone.astype(jnp.float32), axis=0) / total_rows
    eye = jnp.eye(emb, dtype=jnp.float32)
    covariance = (
        jnp.dot(everyone.T, everyone, preferred_element_type=jnp.float32) / total_rows
        - average[:, None] * average[None, :]
        + RIDGE_TERM * eye
    )
    magnitude = jnp.sqrt(jnp.sum(covariance * covariance))
    s1 = eye - (2.0 / magnitude) * covariance
    s2 = fdot(s1, s1)
    s4 = fdot(s2, s2)
    rows = (embedded - average) * (2.0 / magnitude)
    rows = rows + fdot(rows, s1)
    rows = rows + fdot(rows, s2)
    rows = rows + fdot(rows, s4)
    rows = rows + fdot(fdot(rows, s4), s4)
    whitened = rows.astype(jnp.bfloat16)
    capacity = 2 * pass_rows // n_dp
    target_owner = owners[:, 0]
    position = lax.broadcasted_iota(jnp.int32, (pass_rows, pass_rows), 0)
    previous = lax.broadcasted_iota(jnp.int32, (pass_rows, pass_rows), 1)
    earlier = (target_owner[:, None] == target_owner[None, :]) & (previous < position)
    target = target_owner * capacity + jnp.sum(earlier.astype(jnp.int32), axis=1)
    slot_index = lax.broadcasted_iota(jnp.int32, (n_dp * capacity, pass_rows), 0)
    selector = (slot_index == target[None, :]).astype(jnp.bfloat16)
    outgoing = jnp.dot(selector, whitened, preferred_element_type=jnp.float32).astype(jnp.bfloat16)
    return lax.all_to_all(outgoing, "dp", split_axis=0, concat_axis=0, tiled=True)


def solution(mesh):
    placed = (
        P(("dp", "fsdp"), None),
        P(("dp", "fsdp")),
        P(),
        P("fsdp", None),
        P("fsdp", None),
        P(),
        P("fsdp", None),
        P(("dp", "fsdp"), None),
    )
    return jax.shard_map(
        on_device, mesh=mesh, in_specs=placed, out_specs=P(("dp", "fsdp"), None), check_vma=False
    )
```

```python
import functools

import jax
import jax.numpy as jnp
from jax import lax
from jax.experimental import pallas as pl
from jax.experimental.pallas import tpu as pltpu
from jax.sharding import PartitionSpec as P

RIDGE_TERM = 1.0
EPSILON = 1e-06
HIGH = lax.Precision.HIGH


def fdot(a, b):
    return jnp.dot(a, b, precision=HIGH, preferred_element_type=jnp.float32)


MESH = pl.DeviceIdType.MESH
PLANE = 4


def remote(src, dst, send, recv, device):
    return pltpu.make_async_remote_copy(
        src_ref=src, dst_ref=dst, send_sem=send, recv_sem=recv, device_id=device, device_id_type=MESH
    )


def meet(devices):
    barrier = pltpu.get_barrier_semaphore()
    for device in devices:
        pl.semaphore_signal(barrier, inc=1, device_id=device, device_id_type=MESH)
    pl.semaphore_wait(barrier, len(devices))


def mate(q, e):
    if e == 1:
        return q + 1 - 2 * (q % 2)
    if e == 2:
        return q + 2 - 4 * (q // 2)
    return 3 - q


def gather_kernel(
    nz, up_ref, full_ref, own_sem, z_send, z_recv, p_send, p_recv, x_send, x_recv, f_send, f_recv
):
    i = lax.axis_index("dp")
    j = lax.axis_index("fsdp")
    z = j // 2
    c = j % 2
    q = i % PLANE
    base = i - q
    rows = up_ref.shape[0]
    cols = up_ref.shape[1] // PLANE

    def row_at(level):
        return pl.ds(pl.multiple_of((level * 2 + c) * rows, rows), rows)

    def col_at(part):
        return pl.ds(pl.multiple_of(part * cols, cols), cols)

    partner = (i, z * 2 + 1 - c)
    z_peers = [(i, ((z + d) % nz) * 2 + c) for d in range(1, nz)]
    mates = [(base + mate(q, e), j) for e in range(1, 3)]
    meet([partner] + z_peers + mates)
    own = pltpu.make_async_copy(up_ref, full_ref.at[row_at(z), :], own_sem)
    pending = []

    def send(src, dst, ssem, rsem, device):
        copy = remote(src, dst, ssem, rsem, device)
        copy.start()
        pending.append(copy)
        return copy

    z_copies = [
        send(
            up_ref.at[:, col_at(q)], full_ref.at[row_at(z), col_at(q)], z_send.at[d], z_recv.at[d], peer
        )
        for d, peer in enumerate(z_peers)
    ]
    own.start()
    p_copies = [send(up_ref, full_ref.at[row_at(z), :], p_send, p_recv, partner)]
    near_x, near_y = mates[0], mates[1]
    half = rows // 2

    def half_at(level, part):
        return pl.ds(pl.multiple_of((level * 2 + c) * rows + part * half, half), half)

    def forward(piece, n):
        p_copies.append(send(piece, piece, f_send.at[n], f_recv.at[n], partner))

    levels = [(z + nz - d - 1) % nz for d in range(nz - 1)]
    direct = []
    for d, level in enumerate(levels):
        z_copies[d].wait_recv()
        piece = full_ref.at[row_at(level), col_at(q)]
        for e in range(2):
            n = d * 4 + e
            direct.append(send(piece, piece, x_send.at[n], x_recv.at[n], mates[e]))
        forward(piece, d * 5)
    relays = []
    for d, level in enumerate(levels):
        for e in range(2):
            direct[d * 2 + e].wait_recv()
            side = col_at(mate(q, e + 1))
            piece = full_ref.at[half_at(level, e), side]
            n = d * 4 + 2 + e
            to = near_y if e == 0 else near_x
            relays.append(send(piece, piece, x_send.at[n], x_recv.at[n], to))
            forward(full_ref.at[row_at(level), side], d * 5 + 1 + e)
    for d, level in enumerate(levels):
        for e in range(2):
            relays[d * 2 + e].wait_recv()
            forward(full_ref.at[half_at(level, e), col_at(mate(q, 3))], d * 5 + 3 + e)
    for copy in p_copies:
        copy.wait_recv()
    for copy in pending:
        copy.wait_send()
    own.wait()


def gather_up(up_weight, n_fsdp):
    rows, cols = up_weight.shape
    nz = n_fsdp // 2
    dma = pltpu.SemaphoreType.DMA
    return pl.pallas_call(
        functools.partial(gather_kernel, nz),
        out_shape=jax.ShapeDtypeStruct((rows * n_fsdp, cols), up_weight.dtype),
        in_specs=[pl.BlockSpec(memory_space=pl.ANY)],
        out_specs=pl.BlockSpec(memory_space=pl.ANY),
        scratch_shapes=[
            dma,
            dma((nz - 1,)),
            dma((nz - 1,)),
            dma,
            dma,
            dma(((nz - 1) * 4,)),
            dma(((nz - 1) * 4,)),
            dma(((nz - 1) * 5,)),
            dma(((nz - 1) * 5,)),
        ],
        compiler_params=pltpu.CompilerParams(collective_id=0, has_side_effects=True),
        name="gather_up",
    )(up_weight)


def mix_kernel(
    n_dp, n_fsdp, width,
    a_ref, h_ref, down_ref, proj_ref, gain_ref, emb_ref, all_ref,
    ra, rh, pj, sp, rp, s2, r2, s3, r3,
    as_, ar, hs, hr, s2s, r2s, s3s, r3s, es, er, ps, pr, qs, qr, cs, cr,
):
    i = lax.axis_index("dp")
    j = lax.axis_index("fsdp")
    nz = n_fsdp // 2
    z = j // 2
    c = j % 2
    partner = (i, z * 2 + 1 - c)
    peers = [(j + d) % n_fsdp for d in range(1, n_fsdp)]
    levels = [(z + d) % nz for d in range(1, nz)]
    planes = [(i + e) % n_dp for e in range(1, n_dp)]
    pass_rows, ff_rows = a_ref.shape[1:]
    cols = h_ref.shape[2]
    emb = proj_ref.shape[1]
    half = nz * pass_rows
    slot = c * nz + z
    meet([(i, p) for p in peers] + [(p, j) for p in planes])
    pending = []

    def send(src, dst, ssem, rsem, device):
        copy = remote(src, dst, ssem, rsem, device)
        copy.start()
        pending.append(copy)
        return copy

    def along(level):
        return (i, level * 2 + c)

    first = []
    for d, p in enumerate(peers):
        first.append(send(a_ref.at[p], ra.at[slot], as_.at[d], ar.at[d], (i, p)))
    second = []
    for d, v in enumerate(levels):
        second.append(send(h_ref.at[v], rh.at[z], hs.at[d], hr.at[d], along(v)))
    proj_copy = send(proj_ref, pj.at[c], cs.at[0], cr.at[0], partner)
    pj[c] = proj_ref[...]
    ra[slot] = a_ref[j]
    rh[z] = h_ref[z]
    for copy in first:
        copy.wait_recv()

    def share(core):
        rows = ra[pl.ds(core * nz, nz)].reshape(half, ff_rows)
        return jnp.dot(rows, down_ref[...], preferred_element_type=jnp.float32)

    sp[...] = share(1 - c).astype(sp.dtype)
    swap = send(sp, rp, cs.at[1], cr.at[1], partner)
    mine = share(c)
    swap.wait_recv()
    mine = mine + rp[...].astype(jnp.float32)
    for v in range(nz):
        s2[v] = mine[:, v * cols : (v + 1) * cols].astype(s2.dtype)
    parts = [
        send(s2.at[v], r2.at[d], s2s.at[d], r2s.at[d], along(v)) for d, v in enumerate(levels)
    ]
    for copy in second:
        copy.wait_recv()
    pooled = s2[z].astype(jnp.float32) + rh[...].astype(jnp.float32).reshape(half, cols)
    proj_copy.wait_recv()
    for d, copy in enumerate(parts):
        copy.wait_recv()
        pooled = pooled + r2[d].astype(jnp.float32)
    squares = jnp.sum(pooled * pooled, axis=1, keepdims=True)
    scaled = (pooled * gain_ref[...]).astype(proj_ref.dtype)
    part = jnp.dot(scaled, pj[...].reshape(cols, emb), preferred_element_type=jnp.float32)
    s3[:, :, :emb] = part.astype(s3.dtype).reshape(nz, pass_rows, emb)
    wide = jnp.broadcast_to(squares, (half, 128))
    high = wide.astype(s3.dtype)
    low = (wide - high.astype(jnp.float32)).astype(s3.dtype)
    s3[:, :, emb : emb + 128] = high.reshape(nz, pass_rows, 128)
    s3[:, :, emb + 128 : emb + 256] = low.reshape(nz, pass_rows, 128)
    third = [
        send(s3.at[v], r3.at[d], s3s.at[d], r3s.at[d], along(v)) for d, v in enumerate(levels)
    ]
    total = s3[z].astype(jnp.float32)
    for d, copy in enumerate(third):
        copy.wait_recv()
        total = total + r3[d].astype(jnp.float32)
    norm = (total[:, emb : emb + 1] + total[:, emb + 128 : emb + 129]) / width
    embedded = total[:, :emb] * lax.rsqrt(norm + EPSILON)
    emb_ref[...] = embedded
    all_ref[i, c, z] = embedded.astype(all_ref.dtype)
    mine_rows = all_ref.at[i, c, z]
    fourth = [
        send(mine_rows, mine_rows, es.at[d], er.at[d], along(v)) for d, v in enumerate(levels)
    ]
    for copy in fourth:
        copy.wait_recv()
    block = all_ref.at[i, c]
    fifth = [send(block, block, ps.at[e], pr.at[e], (p, j)) for e, p in enumerate(planes)]
    last = [send(block, block, qs.at[0], qr.at[0], partner)]
    for e, copy in enumerate(fifth):
        copy.wait_recv()
        piece = all_ref.at[(i + n_dp - e - 1) % n_dp, c]
        last.append(send(piece, piece, qs.at[e + 1], qr.at[e + 1], partner))
    for copy in last:
        copy.wait_recv()
    for copy in pending:
        copy.wait_send()


def mix(acts, hid, down, proj, gain, n_dp):
    n_fsdp, pass_rows, ff_rows = acts.shape
    nz = n_fsdp // 2
    d_rows, emb = proj.shape
    cols = 2 * d_rows
    half = nz * pass_rows
    width = down.shape[1]
    bf = jnp.bfloat16
    dma = pltpu.SemaphoreType.DMA
    vmem = pl.BlockSpec(memory_space=pltpu.VMEM)
    return pl.pallas_call(
        functools.partial(mix_kernel, n_dp, n_fsdp, float(width)),
        out_shape=(
            jax.ShapeDtypeStruct((pass_rows, emb), jnp.float32),
            jax.ShapeDtypeStruct((n_dp, 2, nz, pass_rows, emb), bf),
        ),
        in_specs=[vmem] * 5,
        out_specs=(vmem, vmem),
        scratch_shapes=[
            pltpu.VMEM((n_fsdp, pass_rows, ff_rows), bf),
            pltpu.VMEM((nz, pass_rows, cols), bf),
            pltpu.VMEM((2, d_rows, emb), bf),
            pltpu.VMEM((half, width), bf),
            pltpu.VMEM((half, width), bf),
            pltpu.VMEM((nz, half, cols), bf),
            pltpu.VMEM((nz - 1, half, cols), bf),
            pltpu.VMEM((nz, pass_rows, emb + 256), bf),
            pltpu.VMEM((nz - 1, pass_rows, emb + 256), bf),
        ]
        + [dma((n_fsdp - 1,))] * 2
        + [dma((nz - 1,))] * 8
        + [dma((n_dp - 1,))] * 2
        + [dma((n_dp,))] * 2
        + [dma((2,))] * 2,
        compiler_params=pltpu.CompilerParams(
            collective_id=1, has_side_effects=True, vmem_limit_bytes=40 * 1024 * 1024
        ),
        name="mix",
    )(acts, hid, down, proj, gain)


def on_device(hidden, lengths, norm_gain, up_weight, down_weight, pool_gain, proj_weight, owners):
    tok_rows, width = hidden.shape
    pass_rows = lengths.shape[0]
    seq_len = tok_rows // pass_rows
    n_fsdp = lax.axis_size("fsdp")
    n_dp = lax.axis_size("dp")
    me = lax.axis_index("fsdp")
    ff_rows = down_weight.shape[0]
    d_rows, emb = proj_weight.shape
    group = n_fsdp * pass_rows
    hidden32 = hidden.astype(jnp.float32)
    normed = (
        hidden32
        * lax.rsqrt(jnp.mean(hidden32 * hidden32, axis=-1, keepdims=True) + EPSILON)
        * norm_gain
    ).astype(jnp.bfloat16)
    hidden_pre = jnp.dot(
        normed,
        gather_up(up_weight, n_fsdp),
        preferred_element_type=jnp.float32,
    )
    activated = jax.nn.gelu(hidden_pre, approximate=True).astype(jnp.bfloat16)
    token_index = lax.broadcasted_iota(jnp.int32, (pass_rows, tok_rows), 1)
    passage_index = lax.broadcasted_iota(jnp.int32, (pass_rows, tok_rows), 0)
    inside = (
        (token_index // seq_len == passage_index) & (token_index % seq_len < lengths[:, None])
    ).astype(jnp.bfloat16)
    inverse = 1.0 / lengths.astype(jnp.float32)[:, None]
    act_mean = jnp.dot(inside, activated, preferred_element_type=jnp.float32) * inverse
    hid_mean = jnp.dot(inside, hidden, preferred_element_type=jnp.float32) * inverse
    acts = act_mean.astype(jnp.bfloat16).reshape(pass_rows, n_fsdp, ff_rows).transpose(1, 0, 2)
    nz = n_fsdp // 2
    hid = hid_mean.astype(jnp.bfloat16).reshape(pass_rows, nz, 2 * d_rows).transpose(1, 0, 2)
    gain = lax.dynamic_slice(pool_gain, (me // 2 * 2 * d_rows,), (2 * d_rows,))[None, :]
    embedded, everyone = mix(acts, hid, down_weight, proj_weight, gain, n_dp)
    everyone = everyone.reshape(n_dp * group, emb)
    total_rows = float(everyone.shape[0])
    average = jnp.sum(everyone.astype(jnp.float32), axis=0) / total_rows
    eye = jnp.eye(emb, dtype=jnp.float32)
    covariance = (
        jnp.dot(everyone.T, everyone, preferred_element_type=jnp.float32) / total_rows
        - average[:, None] * average[None, :]
        + RIDGE_TERM * eye
    )
    magnitude = jnp.sqrt(jnp.sum(covariance * covariance))
    s1 = eye - (2.0 / magnitude) * covariance
    s2 = fdot(s1, s1)
    s4 = fdot(s2, s2)
    rows = (embedded - average) * (2.0 / magnitude)
    rows = rows + fdot(rows, s1)
    rows = rows + fdot(rows, s2)
    rows = rows + fdot(rows, s4)
    rows = rows + fdot(fdot(rows, s4), s4)
    whitened = rows.astype(jnp.bfloat16)
    capacity = 2 * pass_rows // n_dp
    target_owner = owners[:, 0]
    position = lax.broadcasted_iota(jnp.int32, (pass_rows, pass_rows), 0)
    previous = lax.broadcasted_iota(jnp.int32, (pass_rows, pass_rows), 1)
    earlier = (target_owner[:, None] == target_owner[None, :]) & (previous < position)
    target = target_owner * capacity + jnp.sum(earlier.astype(jnp.int32), axis=1)
    slot_index = lax.broadcasted_iota(jnp.int32, (n_dp * capacity, pass_rows), 0)
    selector = (slot_index == target[None, :]).astype(jnp.bfloat16)
    outgoing = jnp.dot(selector, whitened, preferred_element_type=jnp.float32).astype(jnp.bfloat16)
    return lax.all_to_all(outgoing, "dp", split_axis=0, concat_axis=0, tiled=True)


def solution(mesh):
    placed = (
        P(("dp", "fsdp"), None),
        P(("dp", "fsdp")),
        P(),
        P("fsdp", None),
        P("fsdp", None),
        P(),
        P("fsdp", None),
        P(("dp", "fsdp"), None),
    )
    return jax.shard_map(
        on_device, mesh=mesh, in_specs=placed, out_specs=P(("dp", "fsdp"), None), check_vma=False
    )
```

```python
import functools

import jax
import jax.numpy as jnp
from jax import lax
from jax.experimental import pallas as pl
from jax.experimental.pallas import tpu as pltpu
from jax.sharding import PartitionSpec as P

RIDGE_TERM = 1.0
EPSILON = 1e-06
HIGH = lax.Precision.HIGH


def fdot(a, b):
    return jnp.dot(a, b, precision=HIGH, preferred_element_type=jnp.float32)


MESH = pl.DeviceIdType.MESH
PLANE = 4
CHUNKS = 3


def remote(src, dst, send, recv, device):
    return pltpu.make_async_remote_copy(
        src_ref=src, dst_ref=dst, send_sem=send, recv_sem=recv, device_id=device, device_id_type=MESH
    )


def meet(devices):
    barrier = pltpu.get_barrier_semaphore()
    for device in devices:
        pl.semaphore_signal(barrier, inc=1, device_id=device, device_id_type=MESH)
    pl.semaphore_wait(barrier, len(devices))


def mate(q, e):
    if e == 1:
        return q + 1 - 2 * (q % 2)
    if e == 2:
        return q + 2 - 4 * (q // 2)
    return 3 - q


def gather_kernel(
    nz, up_ref, full_ref, own_sem, z_send, z_recv, p_send, p_recv, x_send, x_recv, f_send, f_recv
):
    i = lax.axis_index("dp")
    j = lax.axis_index("fsdp")
    z = j // 2
    c = j % 2
    q = i % PLANE
    base = i - q
    rows = up_ref.shape[0]
    cols = up_ref.shape[1] // PLANE

    def row_at(level):
        return pl.ds(pl.multiple_of((level * 2 + c) * rows, rows), rows)

    def col_at(part):
        return pl.ds(pl.multiple_of(part * cols, cols), cols)

    partner = (i, z * 2 + 1 - c)
    z_peers = [(i, ((z + d) % nz) * 2 + c) for d in range(1, nz)]
    mates = [(base + mate(q, e), j) for e in range(1, 3)]
    meet([partner] + z_peers + mates)
    own = pltpu.make_async_copy(up_ref, full_ref.at[row_at(z), :], own_sem)
    pending = []

    def send(src, dst, ssem, rsem, device):
        copy = remote(src, dst, ssem, rsem, device)
        copy.start()
        pending.append(copy)
        return copy

    near_x, near_y = mates[0], mates[1]
    half = rows // 2
    chunk = cols // CHUNKS

    def half_at(level, part):
        return pl.ds(pl.multiple_of((level * 2 + c) * rows + part * half, half), half)

    def chunk_at(part, ch):
        return pl.ds(pl.multiple_of(part * cols + ch * chunk, chunk), chunk)

    z_copies = {}
    direct = {}
    relays = {}
    p_copies = []

    def start_z(ch):
        for d, peer in enumerate(z_peers):
            n = ch * (nz - 1) + d
            src = up_ref.at[:, chunk_at(q, ch)]
            dst = full_ref.at[row_at(z), chunk_at(q, ch)]
            z_copies[ch, d] = send(src, dst, z_send.at[n], z_recv.at[n], peer)

    def forward(piece, n):
        p_copies.append(send(piece, piece, f_send.at[n], f_recv.at[n], partner))

    levels = [(z + nz - d - 1) % nz for d in range(nz - 1)]

    def spread(ch):
        for d, level in enumerate(levels):
            z_copies[ch, d].wait_recv()
            piece = full_ref.at[row_at(level), chunk_at(q, ch)]
            for e in range(2):
                n = (ch * (nz - 1) + d) * 4 + e
                direct[ch, d, e] = send(piece, piece, x_send.at[n], x_recv.at[n], mates[e])
            forward(piece, (ch * (nz - 1) + d) * 5)
        if ch + 2 < CHUNKS:
            start_z(ch + 2)

    def relay(ch):
        for d, level in enumerate(levels):
            for e in range(2):
                direct[ch, d, e].wait_recv()
                side = chunk_at(mate(q, e + 1), ch)
                piece = full_ref.at[half_at(level, e), side]
                n = (ch * (nz - 1) + d) * 4 + 2 + e
                to = near_y if e == 0 else near_x
                relays[ch, d, e] = send(piece, piece, x_send.at[n], x_recv.at[n], to)
                forward(full_ref.at[row_at(level), side], (ch * (nz - 1) + d) * 5 + 1 + e)

    def finish(ch):
        for d, level in enumerate(levels):
            for e in range(2):
                relays[ch, d, e].wait_recv()
                piece = full_ref.at[half_at(level, e), chunk_at(mate(q, 3), ch)]
                forward(piece, (ch * (nz - 1) + d) * 5 + 3 + e)

    start_z(0)
    start_z(1)
    own.start()
    p_copies.append(send(up_ref, full_ref.at[row_at(z), :], p_send, p_recv, partner))
    for step in range(CHUNKS + 2):
        if step < CHUNKS:
            spread(step)
        if 0 <= step - 1 < CHUNKS:
            relay(step - 1)
        if step >= 2:
            finish(step - 2)
    for copy in p_copies:
        copy.wait_recv()
    for copy in pending:
        copy.wait_send()
    own.wait()


def gather_up(up_weight, n_fsdp):
    rows, cols = up_weight.shape
    nz = n_fsdp // 2
    dma = pltpu.SemaphoreType.DMA
    return pl.pallas_call(
        functools.partial(gather_kernel, nz),
        out_shape=jax.ShapeDtypeStruct((rows * n_fsdp, cols), up_weight.dtype),
        in_specs=[pl.BlockSpec(memory_space=pl.ANY)],
        out_specs=pl.BlockSpec(memory_space=pl.ANY),
        scratch_shapes=[
            dma,
            dma((CHUNKS * (nz - 1),)),
            dma((CHUNKS * (nz - 1),)),
            dma,
            dma,
            dma((CHUNKS * (nz - 1) * 4,)),
            dma((CHUNKS * (nz - 1) * 4,)),
            dma((CHUNKS * (nz - 1) * 5,)),
            dma((CHUNKS * (nz - 1) * 5,)),
        ],
        compiler_params=pltpu.CompilerParams(collective_id=0, has_side_effects=True),
        name="gather_up",
    )(up_weight)


def mix_kernel(
    n_dp, n_fsdp, width,
    a_ref, h_ref, down_ref, proj_ref, gain_ref, emb_ref, all_ref,
    ra, rh, pj, sp, rp, s2, r2, s3, r3,
    as_, ar, hs, hr, s2s, r2s, s3s, r3s, es, er, ps, pr, qs, qr, cs, cr,
):
    i = lax.axis_index("dp")
    j = lax.axis_index("fsdp")
    nz = n_fsdp // 2
    z = j // 2
    c = j % 2
    partner = (i, z * 2 + 1 - c)
    peers = [(j + d) % n_fsdp for d in range(1, n_fsdp)]
    levels = [(z + d) % nz for d in range(1, nz)]
    planes = [(i + e) % n_dp for e in range(1, n_dp)]
    pass_rows, ff_rows = a_ref.shape[1:]
    cols = h_ref.shape[2]
    emb = proj_ref.shape[1]
    half = nz * pass_rows
    slot = c * nz + z
    meet([(i, p) for p in peers] + [(p, j) for p in planes])
    pending = []

    def send(src, dst, ssem, rsem, device):
        copy = remote(src, dst, ssem, rsem, device)
        copy.start()
        pending.append(copy)
        return copy

    def along(level):
        return (i, level * 2 + c)

    first = []
    for d, p in enumerate(peers):
        first.append(send(a_ref.at[p], ra.at[slot], as_.at[d], ar.at[d], (i, p)))
    second = []
    for d, v in enumerate(levels):
        second.append(send(h_ref.at[v], rh.at[z], hs.at[d], hr.at[d], along(v)))
    proj_copy = send(proj_ref, pj.at[c], cs.at[0], cr.at[0], partner)
    pj[c] = proj_ref[...]
    ra[slot] = a_ref[j]
    rh[z] = h_ref[z]
    for copy in first:
        copy.wait_recv()

    def share(core):
        rows = ra[pl.ds(core * nz, nz)].reshape(half, ff_rows)
        return jnp.dot(rows, down_ref[...], preferred_element_type=jnp.float32)

    sp[...] = share(1 - c).astype(sp.dtype)
    swap = send(sp, rp, cs.at[1], cr.at[1], partner)
    mine = share(c)
    swap.wait_recv()
    mine = mine + rp[...].astype(jnp.float32)
    for v in range(nz):
        s2[v] = mine[:, v * cols : (v + 1) * cols].astype(s2.dtype)
    parts = [
        send(s2.at[v], r2.at[d], s2s.at[d], r2s.at[d], along(v)) for d, v in enumerate(levels)
    ]
    for copy in second:
        copy.wait_recv()
    pooled = s2[z].astype(jnp.float32) + rh[...].astype(jnp.float32).reshape(half, cols)
    proj_copy.wait_recv()
    for d, copy in enumerate(parts):
        copy.wait_recv()
        pooled = pooled + r2[d].astype(jnp.float32)
    squares = jnp.sum(pooled * pooled, axis=1, keepdims=True)
    scaled = (pooled * gain_ref[...]).astype(proj_ref.dtype)
    part = jnp.dot(scaled, pj[...].reshape(cols, emb), preferred_element_type=jnp.float32)
    s3[:, :, :emb] = part.astype(s3.dtype).reshape(nz, pass_rows, emb)
    wide = jnp.broadcast_to(squares, (half, 128))
    high = wide.astype(s3.dtype)
    low = (wide - high.astype(jnp.float32)).astype(s3.dtype)
    s3[:, :, emb : emb + 128] = high.reshape(nz, pass_rows, 128)
    s3[:, :, emb + 128 : emb + 256] = low.reshape(nz, pass_rows, 128)
    third = [
        send(s3.at[v], r3.at[d], s3s.at[d], r3s.at[d], along(v)) for d, v in enumerate(levels)
    ]
    total = s3[z].astype(jnp.float32)
    for d, copy in enumerate(third):
        copy.wait_recv()
        total = total + r3[d].astype(jnp.float32)
    norm = (total[:, emb : emb + 1] + total[:, emb + 128 : emb + 129]) / width
    embedded = total[:, :emb] * lax.rsqrt(norm + EPSILON)
    emb_ref[...] = embedded
    all_ref[i, c, z] = embedded.astype(all_ref.dtype)
    mine_rows = all_ref.at[i, c, z]
    fourth = [
        send(mine_rows, mine_rows, es.at[d], er.at[d], along(v)) for d, v in enumerate(levels)
    ]
    for copy in fourth:
        copy.wait_recv()
    block = all_ref.at[i, c]
    fifth = [send(block, block, ps.at[e], pr.at[e], (p, j)) for e, p in enumerate(planes)]
    last = [send(block, block, qs.at[0], qr.at[0], partner)]
    for e, copy in enumerate(fifth):
        copy.wait_recv()
        piece = all_ref.at[(i + n_dp - e - 1) % n_dp, c]
        last.append(send(piece, piece, qs.at[e + 1], qr.at[e + 1], partner))
    for copy in last:
        copy.wait_recv()
    for copy in pending:
        copy.wait_send()


def mix(acts, hid, down, proj, gain, n_dp):
    n_fsdp, pass_rows, ff_rows = acts.shape
    nz = n_fsdp // 2
    d_rows, emb = proj.shape
    cols = 2 * d_rows
    half = nz * pass_rows
    width = down.shape[1]
    bf = jnp.bfloat16
    dma = pltpu.SemaphoreType.DMA
    vmem = pl.BlockSpec(memory_space=pltpu.VMEM)
    return pl.pallas_call(
        functools.partial(mix_kernel, n_dp, n_fsdp, float(width)),
        out_shape=(
            jax.ShapeDtypeStruct((pass_rows, emb), jnp.float32),
            jax.ShapeDtypeStruct((n_dp, 2, nz, pass_rows, emb), bf),
        ),
        in_specs=[vmem] * 5,
        out_specs=(vmem, vmem),
        scratch_shapes=[
            pltpu.VMEM((n_fsdp, pass_rows, ff_rows), bf),
            pltpu.VMEM((nz, pass_rows, cols), bf),
            pltpu.VMEM((2, d_rows, emb), bf),
            pltpu.VMEM((half, width), bf),
            pltpu.VMEM((half, width), bf),
            pltpu.VMEM((nz, half, cols), bf),
            pltpu.VMEM((nz - 1, half, cols), bf),
            pltpu.VMEM((nz, pass_rows, emb + 256), bf),
            pltpu.VMEM((nz - 1, pass_rows, emb + 256), bf),
        ]
        + [dma((n_fsdp - 1,))] * 2
        + [dma((nz - 1,))] * 8
        + [dma((n_dp - 1,))] * 2
        + [dma((n_dp,))] * 2
        + [dma((2,))] * 2,
        compiler_params=pltpu.CompilerParams(
            collective_id=1, has_side_effects=True, vmem_limit_bytes=40 * 1024 * 1024
        ),
        name="mix",
    )(acts, hid, down, proj, gain)


def route_kernel(n_dp, out_ref, in_ref, ssem, rsem):
    i = lax.axis_index("dp")
    j = lax.axis_index("fsdp")
    planes = [(i + e) % n_dp for e in range(1, n_dp)]
    meet([(p, j) for p in planes])
    copies = []
    for e, p in enumerate(planes):
        copy = remote(out_ref.at[p], in_ref.at[i], ssem.at[e], rsem.at[e], (p, j))
        copy.start()
        copies.append(copy)
    in_ref[i] = out_ref[i]
    for copy in copies:
        copy.wait()


def route(outgoing, n_dp):
    vmem = pl.BlockSpec(memory_space=pltpu.VMEM)
    return pl.pallas_call(
        functools.partial(route_kernel, n_dp),
        out_shape=jax.ShapeDtypeStruct(outgoing.shape, outgoing.dtype),
        in_specs=[vmem],
        out_specs=vmem,
        scratch_shapes=[pltpu.SemaphoreType.DMA((n_dp - 1,))] * 2,
        compiler_params=pltpu.CompilerParams(collective_id=2, has_side_effects=True),
        name="route",
    )(outgoing)


def on_device(hidden, lengths, norm_gain, up_weight, down_weight, pool_gain, proj_weight, owners):
    tok_rows, width = hidden.shape
    pass_rows = lengths.shape[0]
    seq_len = tok_rows // pass_rows
    n_fsdp = lax.axis_size("fsdp")
    n_dp = lax.axis_size("dp")
    me = lax.axis_index("fsdp")
    ff_rows = down_weight.shape[0]
    d_rows, emb = proj_weight.shape
    group = n_fsdp * pass_rows
    hidden32 = hidden.astype(jnp.float32)
    normed = (
        hidden32
        * lax.rsqrt(jnp.mean(hidden32 * hidden32, axis=-1, keepdims=True) + EPSILON)
        * norm_gain
    ).astype(jnp.bfloat16)
    hidden_pre = jnp.dot(
        normed,
        gather_up(up_weight, n_fsdp),
        preferred_element_type=jnp.float32,
    )
    activated = jax.nn.gelu(hidden_pre, approximate=True).astype(jnp.bfloat16)
    token_index = lax.broadcasted_iota(jnp.int32, (pass_rows, tok_rows), 1)
    passage_index = lax.broadcasted_iota(jnp.int32, (pass_rows, tok_rows), 0)
    inside = (
        (token_index // seq_len == passage_index) & (token_index % seq_len < lengths[:, None])
    ).astype(jnp.bfloat16)
    inverse = 1.0 / lengths.astype(jnp.float32)[:, None]
    act_mean = jnp.dot(inside, activated, preferred_element_type=jnp.float32) * inverse
    hid_mean = jnp.dot(inside, hidden, preferred_element_type=jnp.float32) * inverse
    acts = act_mean.astype(jnp.bfloat16).reshape(pass_rows, n_fsdp, ff_rows).transpose(1, 0, 2)
    nz = n_fsdp // 2
    hid = hid_mean.astype(jnp.bfloat16).reshape(pass_rows, nz, 2 * d_rows).transpose(1, 0, 2)
    gain = lax.dynamic_slice(pool_gain, (me // 2 * 2 * d_rows,), (2 * d_rows,))[None, :]
    embedded, everyone = mix(acts, hid, down_weight, proj_weight, gain, n_dp)
    everyone = everyone.reshape(n_dp * group, emb)
    total_rows = float(everyone.shape[0])
    average = jnp.sum(everyone.astype(jnp.float32), axis=0) / total_rows
    eye = jnp.eye(emb, dtype=jnp.float32)
    covariance = (
        jnp.dot(everyone.T, everyone, preferred_element_type=jnp.float32) / total_rows
        - average[:, None] * average[None, :]
        + RIDGE_TERM * eye
    )
    magnitude = jnp.sqrt(jnp.sum(covariance * covariance))
    s1 = eye - (2.0 / magnitude) * covariance
    s2 = fdot(s1, s1)
    s4 = fdot(s2, s2)
    rows = (embedded - average) * (2.0 / magnitude)
    rows = rows + fdot(rows, s1)
    rows = rows + fdot(rows, s2)
    rows = rows + fdot(rows, s4)
    rows = rows + fdot(fdot(rows, s4), s4)
    whitened = rows.astype(jnp.bfloat16)
    capacity = 2 * pass_rows // n_dp
    target_owner = owners[:, 0]
    position = lax.broadcasted_iota(jnp.int32, (pass_rows, pass_rows), 0)
    previous = lax.broadcasted_iota(jnp.int32, (pass_rows, pass_rows), 1)
    earlier = (target_owner[:, None] == target_owner[None, :]) & (previous < position)
    target = target_owner * capacity + jnp.sum(earlier.astype(jnp.int32), axis=1)
    slot_index = lax.broadcasted_iota(jnp.int32, (n_dp * capacity, pass_rows), 0)
    selector = (slot_index == target[None, :]).astype(jnp.bfloat16)
    outgoing = jnp.dot(selector, whitened, preferred_element_type=jnp.float32).astype(jnp.bfloat16)
    owned = route(outgoing.reshape(n_dp, capacity, emb), n_dp)
    return owned.reshape(n_dp * capacity, emb)


def solution(mesh):
    placed = (
        P(("dp", "fsdp"), None),
        P(("dp", "fsdp")),
        P(),
        P("fsdp", None),
        P("fsdp", None),
        P(),
        P("fsdp", None),
        P(("dp", "fsdp"), None),
    )
    return jax.shard_map(
        on_device, mesh=mesh, in_specs=placed, out_specs=P(("dp", "fsdp"), None), check_vma=False
    )
```

```python
import functools

import jax
import jax.numpy as jnp
from jax import lax
from jax.experimental import pallas as pl
from jax.experimental.pallas import tpu as pltpu
from jax.sharding import PartitionSpec as P

RIDGE_TERM = 1.0
EPSILON = 1e-06
HIGH = lax.Precision.HIGH


def fdot(a, b):
    return jnp.dot(a, b, precision=HIGH, preferred_element_type=jnp.float32)


MESH = pl.DeviceIdType.MESH
PLANE = 4
CHUNKS = 3


def remote(src, dst, send, recv, device):
    return pltpu.make_async_remote_copy(
        src_ref=src, dst_ref=dst, send_sem=send, recv_sem=recv, device_id=device, device_id_type=MESH
    )


def meet(devices):
    barrier = pltpu.get_barrier_semaphore()
    for device in devices:
        pl.semaphore_signal(barrier, inc=1, device_id=device, device_id_type=MESH)
    pl.semaphore_wait(barrier, len(devices))


def mate(q, e):
    if e == 1:
        return q + 1 - 2 * (q % 2)
    if e == 2:
        return q + 2 - 4 * (q // 2)
    return 3 - q


def gather_kernel(
    nz, up_ref, full_ref, own_sem, z_send, z_recv, p_send, p_recv, x_send, x_recv, f_send, f_recv
):
    i = lax.axis_index("dp")
    j = lax.axis_index("fsdp")
    z = j // 2
    c = j % 2
    q = i % PLANE
    base = i - q
    rows = up_ref.shape[0]
    cols = up_ref.shape[1] // PLANE

    def row_at(level):
        return pl.ds(pl.multiple_of((level * 2 + c) * rows, rows), rows)

    def col_at(part):
        return pl.ds(pl.multiple_of(part * cols, cols), cols)

    partner = (i, z * 2 + 1 - c)
    z_peers = [(i, ((z + d) % nz) * 2 + c) for d in range(1, nz)]
    mates = [(base + mate(q, e), j) for e in range(1, 3)]
    meet([partner] + z_peers + mates)
    own = pltpu.make_async_copy(up_ref, full_ref.at[row_at(z), :], own_sem)
    pending = []

    def send(src, dst, ssem, rsem, device):
        copy = remote(src, dst, ssem, rsem, device)
        copy.start()
        pending.append(copy)
        return copy

    near_x, near_y = mates[0], mates[1]
    half = rows // 2
    chunk = cols // CHUNKS

    def half_at(level, part):
        return pl.ds(pl.multiple_of((level * 2 + c) * rows + part * half, half), half)

    def chunk_at(part, ch):
        return pl.ds(pl.multiple_of(part * cols + ch * chunk, chunk), chunk)

    z_copies = {}
    direct = {}
    relays = {}
    p_copies = []

    def start_z(ch):
        for d, peer in enumerate(z_peers):
            n = ch * (nz - 1) + d
            src = up_ref.at[:, chunk_at(q, ch)]
            dst = full_ref.at[row_at(z), chunk_at(q, ch)]
            z_copies[ch, d] = send(src, dst, z_send.at[n], z_recv.at[n], peer)

    def forward(piece, n):
        p_copies.append(send(piece, piece, f_send.at[n], f_recv.at[n], partner))

    levels = [(z + nz - d - 1) % nz for d in range(nz - 1)]

    def spread(ch):
        for d, level in enumerate(levels):
            z_copies[ch, d].wait_recv()
            piece = full_ref.at[row_at(level), chunk_at(q, ch)]
            for e in range(2):
                n = (ch * (nz - 1) + d) * 4 + e
                direct[ch, d, e] = send(piece, piece, x_send.at[n], x_recv.at[n], mates[e])
            forward(piece, (ch * (nz - 1) + d) * 5)
        if ch + 2 < CHUNKS:
            start_z(ch + 2)

    def relay(ch):
        for d, level in enumerate(levels):
            for e in range(2):
                direct[ch, d, e].wait_recv()
                side = chunk_at(mate(q, e + 1), ch)
                piece = full_ref.at[half_at(level, e), side]
                n = (ch * (nz - 1) + d) * 4 + 2 + e
                to = near_y if e == 0 else near_x
                relays[ch, d, e] = send(piece, piece, x_send.at[n], x_recv.at[n], to)
                forward(full_ref.at[row_at(level), side], (ch * (nz - 1) + d) * 5 + 1 + e)

    def finish(ch):
        for d, level in enumerate(levels):
            for e in range(2):
                relays[ch, d, e].wait_recv()
                piece = full_ref.at[half_at(level, e), chunk_at(mate(q, 3), ch)]
                forward(piece, (ch * (nz - 1) + d) * 5 + 3 + e)

    start_z(0)
    start_z(1)
    for step in range(CHUNKS + 2):
        if step < CHUNKS:
            spread(step)
        if step == 0:
            own.start()
            p_copies.append(send(up_ref, full_ref.at[row_at(z), :], p_send, p_recv, partner))
        if 0 <= step - 1 < CHUNKS:
            relay(step - 1)
        if step >= 2:
            finish(step - 2)
    for copy in p_copies:
        copy.wait_recv()
    for copy in pending:
        copy.wait_send()
    own.wait()


def gather_up(up_weight, n_fsdp):
    rows, cols = up_weight.shape
    nz = n_fsdp // 2
    dma = pltpu.SemaphoreType.DMA
    return pl.pallas_call(
        functools.partial(gather_kernel, nz),
        out_shape=jax.ShapeDtypeStruct((rows * n_fsdp, cols), up_weight.dtype),
        in_specs=[pl.BlockSpec(memory_space=pl.ANY)],
        out_specs=pl.BlockSpec(memory_space=pl.ANY),
        scratch_shapes=[
            dma,
            dma((CHUNKS * (nz - 1),)),
            dma((CHUNKS * (nz - 1),)),
            dma,
            dma,
            dma((CHUNKS * (nz - 1) * 4,)),
            dma((CHUNKS * (nz - 1) * 4,)),
            dma((CHUNKS * (nz - 1) * 5,)),
            dma((CHUNKS * (nz - 1) * 5,)),
        ],
        compiler_params=pltpu.CompilerParams(collective_id=0, has_side_effects=True),
        name="gather_up",
    )(up_weight)


def mix_kernel(
    n_dp, n_fsdp, width,
    a_ref, h_ref, down_ref, proj_ref, gain_ref, emb_ref, all_ref,
    ra, rh, pj, sp, rp, s2, r2, s3, r3,
    as_, ar, hs, hr, s2s, r2s, s3s, r3s, es, er, ps, pr, qs, qr, cs, cr,
):
    i = lax.axis_index("dp")
    j = lax.axis_index("fsdp")
    nz = n_fsdp // 2
    z = j // 2
    c = j % 2
    partner = (i, z * 2 + 1 - c)
    peers = [(j + d) % n_fsdp for d in range(1, n_fsdp)]
    levels = [(z + d) % nz for d in range(1, nz)]
    planes = [(i + e) % n_dp for e in range(1, n_dp)]
    pass_rows, ff_rows = a_ref.shape[1:]
    cols = h_ref.shape[2]
    emb = proj_ref.shape[1]
    half = nz * pass_rows
    slot = c * nz + z
    meet([(i, p) for p in peers] + [(p, j) for p in planes])
    pending = []

    def send(src, dst, ssem, rsem, device):
        copy = remote(src, dst, ssem, rsem, device)
        copy.start()
        pending.append(copy)
        return copy

    def along(level):
        return (i, level * 2 + c)

    first = []
    for d, p in enumerate(peers):
        first.append(send(a_ref.at[p], ra.at[slot], as_.at[d], ar.at[d], (i, p)))
    second = []
    for d, v in enumerate(levels):
        second.append(send(h_ref.at[v], rh.at[z], hs.at[d], hr.at[d], along(v)))
    proj_copy = send(proj_ref, pj.at[c], cs.at[0], cr.at[0], partner)
    pj[c] = proj_ref[...]
    ra[slot] = a_ref[j]
    rh[z] = h_ref[z]
    for copy in first:
        copy.wait_recv()

    def share(core):
        rows = ra[pl.ds(core * nz, nz)].reshape(half, ff_rows)
        return jnp.dot(rows, down_ref[...], preferred_element_type=jnp.float32)

    sp[...] = share(1 - c).astype(sp.dtype)
    swap = send(sp, rp, cs.at[1], cr.at[1], partner)
    mine = share(c)
    swap.wait_recv()
    mine = mine + rp[...].astype(jnp.float32)
    for v in range(nz):
        s2[v] = mine[:, v * cols : (v + 1) * cols].astype(s2.dtype)
    parts = [
        send(s2.at[v], r2.at[d], s2s.at[d], r2s.at[d], along(v)) for d, v in enumerate(levels)
    ]
    for copy in second:
        copy.wait_recv()
    pooled = s2[z].astype(jnp.float32) + rh[...].astype(jnp.float32).reshape(half, cols)
    proj_copy.wait_recv()
    for d, copy in enumerate(parts):
        copy.wait_recv()
        pooled = pooled + r2[d].astype(jnp.float32)
    squares = jnp.sum(pooled * pooled, axis=1, keepdims=True)
    scaled = (pooled * gain_ref[...]).astype(proj_ref.dtype)
    part = jnp.dot(scaled, pj[...].reshape(cols, emb), preferred_element_type=jnp.float32)
    s3[:, :, :emb] = part.astype(s3.dtype).reshape(nz, pass_rows, emb)
    wide = jnp.broadcast_to(squares, (half, 128))
    high = wide.astype(s3.dtype)
    low = (wide - high.astype(jnp.float32)).astype(s3.dtype)
    s3[:, :, emb : emb + 128] = high.reshape(nz, pass_rows, 128)
    s3[:, :, emb + 128 : emb + 256] = low.reshape(nz, pass_rows, 128)
    third = [
        send(s3.at[v], r3.at[d], s3s.at[d], r3s.at[d], along(v)) for d, v in enumerate(levels)
    ]
    total = s3[z].astype(jnp.float32)
    for d, copy in enumerate(third):
        copy.wait_recv()
        total = total + r3[d].astype(jnp.float32)
    norm = (total[:, emb : emb + 1] + total[:, emb + 128 : emb + 129]) / width
    embedded = total[:, :emb] * lax.rsqrt(norm + EPSILON)
    emb_ref[...] = embedded
    all_ref[i, c, z] = embedded.astype(all_ref.dtype)
    mine_rows = all_ref.at[i, c, z]
    fourth = [
        send(mine_rows, mine_rows, es.at[d], er.at[d], along(v)) for d, v in enumerate(levels)
    ]
    for copy in fourth:
        copy.wait_recv()
    block = all_ref.at[i, c]
    fifth = [send(block, block, ps.at[e], pr.at[e], (p, j)) for e, p in enumerate(planes)]
    last = [send(block, block, qs.at[0], qr.at[0], partner)]
    for e, copy in enumerate(fifth):
        copy.wait_recv()
        piece = all_ref.at[(i + n_dp - e - 1) % n_dp, c]
        last.append(send(piece, piece, qs.at[e + 1], qr.at[e + 1], partner))
    for copy in last:
        copy.wait_recv()
    for copy in pending:
        copy.wait_send()


def mix(acts, hid, down, proj, gain, n_dp):
    n_fsdp, pass_rows, ff_rows = acts.shape
    nz = n_fsdp // 2
    d_rows, emb = proj.shape
    cols = 2 * d_rows
    half = nz * pass_rows
    width = down.shape[1]
    bf = jnp.bfloat16
    dma = pltpu.SemaphoreType.DMA
    vmem = pl.BlockSpec(memory_space=pltpu.VMEM)
    return pl.pallas_call(
        functools.partial(mix_kernel, n_dp, n_fsdp, float(width)),
        out_shape=(
            jax.ShapeDtypeStruct((pass_rows, emb), jnp.float32),
            jax.ShapeDtypeStruct((n_dp, 2, nz, pass_rows, emb), bf),
        ),
        in_specs=[vmem] * 5,
        out_specs=(vmem, vmem),
        scratch_shapes=[
            pltpu.VMEM((n_fsdp, pass_rows, ff_rows), bf),
            pltpu.VMEM((nz, pass_rows, cols), bf),
            pltpu.VMEM((2, d_rows, emb), bf),
            pltpu.VMEM((half, width), bf),
            pltpu.VMEM((half, width), bf),
            pltpu.VMEM((nz, half, cols), bf),
            pltpu.VMEM((nz - 1, half, cols), bf),
            pltpu.VMEM((nz, pass_rows, emb + 256), bf),
            pltpu.VMEM((nz - 1, pass_rows, emb + 256), bf),
        ]
        + [dma((n_fsdp - 1,))] * 2
        + [dma((nz - 1,))] * 8
        + [dma((n_dp - 1,))] * 2
        + [dma((n_dp,))] * 2
        + [dma((2,))] * 2,
        compiler_params=pltpu.CompilerParams(
            collective_id=1, has_side_effects=True, vmem_limit_bytes=40 * 1024 * 1024
        ),
        name="mix",
    )(acts, hid, down, proj, gain)


def route_kernel(n_dp, out_ref, in_ref, ssem, rsem):
    i = lax.axis_index("dp")
    j = lax.axis_index("fsdp")
    planes = [(i + e) % n_dp for e in range(1, n_dp)]
    meet([(p, j) for p in planes])
    copies = []
    for e, p in enumerate(planes):
        copy = remote(out_ref.at[p], in_ref.at[i], ssem.at[e], rsem.at[e], (p, j))
        copy.start()
        copies.append(copy)
    in_ref[i] = out_ref[i]
    for copy in copies:
        copy.wait()


def route(outgoing, n_dp):
    vmem = pl.BlockSpec(memory_space=pltpu.VMEM)
    return pl.pallas_call(
        functools.partial(route_kernel, n_dp),
        out_shape=jax.ShapeDtypeStruct(outgoing.shape, outgoing.dtype),
        in_specs=[vmem],
        out_specs=vmem,
        scratch_shapes=[pltpu.SemaphoreType.DMA((n_dp - 1,))] * 2,
        compiler_params=pltpu.CompilerParams(collective_id=2, has_side_effects=True),
        name="route",
    )(outgoing)


def on_device(hidden, lengths, norm_gain, up_weight, down_weight, pool_gain, proj_weight, owners):
    tok_rows, width = hidden.shape
    pass_rows = lengths.shape[0]
    seq_len = tok_rows // pass_rows
    n_fsdp = lax.axis_size("fsdp")
    n_dp = lax.axis_size("dp")
    me = lax.axis_index("fsdp")
    ff_rows = down_weight.shape[0]
    d_rows, emb = proj_weight.shape
    group = n_fsdp * pass_rows
    hidden32 = hidden.astype(jnp.float32)
    normed = (
        hidden32
        * lax.rsqrt(jnp.mean(hidden32 * hidden32, axis=-1, keepdims=True) + EPSILON)
        * norm_gain
    ).astype(jnp.bfloat16)
    hidden_pre = jnp.dot(
        normed,
        gather_up(up_weight, n_fsdp),
        preferred_element_type=jnp.float32,
    )
    activated = jax.nn.gelu(hidden_pre, approximate=True).astype(jnp.bfloat16)
    token_index = lax.broadcasted_iota(jnp.int32, (pass_rows, tok_rows), 1)
    passage_index = lax.broadcasted_iota(jnp.int32, (pass_rows, tok_rows), 0)
    inside = (
        (token_index // seq_len == passage_index) & (token_index % seq_len < lengths[:, None])
    ).astype(jnp.bfloat16)
    inverse = 1.0 / lengths.astype(jnp.float32)[:, None]
    act_mean = jnp.dot(inside, activated, preferred_element_type=jnp.float32) * inverse
    hid_mean = jnp.dot(inside, hidden, preferred_element_type=jnp.float32) * inverse
    acts = act_mean.astype(jnp.bfloat16).reshape(pass_rows, n_fsdp, ff_rows).transpose(1, 0, 2)
    nz = n_fsdp // 2
    hid = hid_mean.astype(jnp.bfloat16).reshape(pass_rows, nz, 2 * d_rows).transpose(1, 0, 2)
    gain = lax.dynamic_slice(pool_gain, (me // 2 * 2 * d_rows,), (2 * d_rows,))[None, :]
    embedded, everyone = mix(acts, hid, down_weight, proj_weight, gain, n_dp)
    everyone = everyone.reshape(n_dp * group, emb)
    total_rows = float(everyone.shape[0])
    average = jnp.sum(everyone.astype(jnp.float32), axis=0) / total_rows
    eye = jnp.eye(emb, dtype=jnp.float32)
    covariance = (
        jnp.dot(everyone.T, everyone, preferred_element_type=jnp.float32) / total_rows
        - average[:, None] * average[None, :]
        + RIDGE_TERM * eye
    )
    magnitude = jnp.sqrt(jnp.sum(covariance * covariance))
    s1 = eye - (2.0 / magnitude) * covariance
    s2 = fdot(s1, s1)
    rows = (embedded - average) * (2.0 / magnitude)
    rows = rows + fdot(rows, s1)
    rows = rows + fdot(rows, s2)
    rows = rows + fdot(fdot(rows, s2), s2)
    eighth = rows
    for _ in range(4):
        eighth = fdot(eighth, s2)
    rows = rows + eighth
    whitened = rows.astype(jnp.bfloat16)
    capacity = 2 * pass_rows // n_dp
    target_owner = owners[:, 0]
    position = lax.broadcasted_iota(jnp.int32, (pass_rows, pass_rows), 0)
    previous = lax.broadcasted_iota(jnp.int32, (pass_rows, pass_rows), 1)
    earlier = (target_owner[:, None] == target_owner[None, :]) & (previous < position)
    target = target_owner * capacity + jnp.sum(earlier.astype(jnp.int32), axis=1)
    slot_index = lax.broadcasted_iota(jnp.int32, (n_dp * capacity, pass_rows), 0)
    selector = (slot_index == target[None, :]).astype(jnp.bfloat16)
    outgoing = jnp.dot(selector, whitened, preferred_element_type=jnp.float32).astype(jnp.bfloat16)
    owned = route(outgoing.reshape(n_dp, capacity, emb), n_dp)
    return owned.reshape(n_dp * capacity, emb)


def solution(mesh):
    placed = (
        P(("dp", "fsdp"), None),
        P(("dp", "fsdp")),
        P(),
        P("fsdp", None),
        P("fsdp", None),
        P(),
        P("fsdp", None),
        P(("dp", "fsdp"), None),
    )
    return jax.shard_map(
        on_device, mesh=mesh, in_specs=placed, out_specs=P(("dp", "fsdp"), None), check_vma=False
    )
```
